128 devices in a mesh: row: 8 (over z, x_hi), col: 16 (over y, x_lo, core).
Axes of the slice: x: 4 (x_hi: 2, x_lo: 2; x = x_hi * 2 + x_lo), y: 4, z: 4, core: 2. Of those that a mesh axis runs over, the one named last changes fastest.
Arguments:
- pair: bfloat16 [1024, 1024, 128], P('row', 'col'), may hold values from -6 to 6
- grad_x: bfloat16 [1024, 1024, 64], P('row', 'col'), may hold values from -0.19921875 to 0.19921875
- norm_gain: float32 [128], replicated, may hold values from 0.1 to 1.9
- norm_bias: float32 [128], replicated, may hold values from -3 to 3
- proj_weight: bfloat16 [128, 256], replicated, may hold values from -0.5 to 0.5
- tile_mask: int32 [8, 8], replicated, may hold values 0 or 1
Outputs:
- grad_pair: bfloat16 [1024, 1024, 128], P('row', 'col')
The draws below stay inside these ranges and needn't reach their ends.
All inputs are finite; a program needn't handle non-finite values.
Results may differ from the reference program's by a relative error of at most 0.012.
Values may be sent and summed in bfloat16 or wider, within the bound.
A program may use at most 128 MiB of HBM per device.

```python
import jax
import jax.numpy as jnp
from jax import lax

C = 128
H = 64
BLK = 128
N = 1024
TILE_R = 128
NB = 8
N_ROW = 8


def plant(drawn, rng, least, top_value):
    longest = drawn.shape.index(max(drawn.shape))
    spots = []
    for shift in (0, 1):
        where = [jax.random.randint(jax.random.fold_in(rng, axis), (), 0, length) for axis, length in enumerate(drawn.shape)]
        where[longest] = (where[longest] + shift) % drawn.shape[longest]
        spots.append(tuple(where))
    return drawn.at[spots[0]].set(least).at[spots[1]].set(top_value)


def shard_levels(key, extent, cuts, low, high):
    level = 1.0
    for dim, blocks in cuts:
        heights = jax.random.uniform(jax.random.fold_in(jax.random.fold_in(key, 6), dim), (blocks,), jnp.float32, low / len(cuts), high / len(cuts))
        level = level * jnp.repeat(jnp.exp(heights), extent[dim] // blocks).reshape((-1,) + (1,) * (len(extent) - 1 - dim))
    return level


def noise(rng, shape, deviation, reach, pieces=(), kind=jnp.bfloat16):
    drawn = deviation * jax.random.normal(rng, shape, jnp.float32)
    if pieces:
        drawn = drawn * shard_levels(rng, shape, pieces, -0.22, 0.18)
    return jnp.clip(drawn, -reach, reach).astype(kind)


def setup_inputs(seed: int = 0) -> dict:
    seeds = jax.random.split(jax.random.key(seed), 7)
    pair = noise(seeds[0], (N, N, C), 1.0, 6.0, ((0, 8), (1, 16)))
    grad_x = noise(seeds[1], (N, N, H), 0.03125, 0.19921875, ((0, 8), (1, 16)))
    norm_gain = jnp.clip(1.0 + 0.18 * jax.random.normal(seeds[2], (C,), jnp.float32), 0.1, 1.9)
    norm_bias = noise(seeds[3], (C,), 0.5, 3.0, (), jnp.float32)
    proj_weight = noise(seeds[4], (C, 4 * H), C ** -0.5, 0.5)
    tile_mask = plant((jax.random.randint(seeds[5], (NB, NB), 0, 4) < 3).astype(jnp.int32), jax.random.fold_in(seeds[5], 1), 0, 1)
    return dict(pair=pair, grad_x=grad_x, norm_gain=norm_gain, norm_bias=norm_bias, proj_weight=proj_weight, tile_mask=tile_mask)


def normalize(pair, norm_gain, norm_bias):
    values = pair.astype(jnp.float32)
    centred = values - lax.optimization_barrier(jnp.mean(values, axis=-1, keepdims=True))
    variance = lax.optimization_barrier(jnp.mean(centred * centred, axis=-1, keepdims=True))
    inverse = lax.rsqrt(variance + 1e-05)
    scaled = centred * inverse
    normed = (scaled * norm_gain + norm_bias).astype(jnp.bfloat16)
    return (scaled, inverse, normed)

def reference(pair, grad_x, norm_gain, norm_bias, proj_weight, tile_mask):
    scaled, inverse, normed = normalize(pair, norm_gain, norm_bias)
    projected = jnp.dot(normed.reshape(N * N, C), proj_weight, preferred_element_type=jnp.float32).reshape(N, N, 4 * H)
    block_ids = (jnp.arange(N) // BLK).astype(jnp.int32)
    valid_tile = tile_mask[block_ids][:, block_ids].astype(jnp.float32)[:, :, None]
    lin_left = projected[:, :, 0:H]
    gate_left = projected[:, :, H:2 * H]
    lin_right = projected[:, :, 2 * H:3 * H]
    gate_right = projected[:, :, 3 * H:4 * H]
    sig_left = jax.nn.sigmoid(gate_left)
    sig_right = jax.nn.sigmoid(gate_right)
    left_act = (valid_tile * sig_left * lin_left).astype(jnp.bfloat16)
    right_act = (valid_tile * sig_right * lin_right).astype(jnp.bfloat16)
    grad_wide = grad_x.astype(jnp.float32)
    left_wide = left_act.astype(jnp.float32)
    grad_left = jnp.einsum('ijc,jkc->ikc', grad_wide, right_act.astype(jnp.float32))

    def add_group(group, total):
        grad_rows = lax.dynamic_slice_in_dim(grad_wide, group * TILE_R, TILE_R, 0)
        left_rows = lax.dynamic_slice_in_dim(left_wide, group * TILE_R, TILE_R, 0)
        partial_sum = jnp.einsum('ijc,ikc->jkc', grad_rows, left_rows).astype(jnp.bfloat16)
        partial_sum = lax.optimization_barrier(partial_sum)
        return total + partial_sum.astype(jnp.float32)
    grad_right = lax.fori_loop(0, N_ROW, add_group, jnp.zeros((N, N, H), jnp.float32))
    grad_proj = jnp.concatenate([grad_left * valid_tile * sig_left, grad_left * valid_tile * lin_left * sig_left * (1.0 - sig_left), grad_right * valid_tile * sig_right, grad_right * valid_tile * lin_right * sig_right * (1.0 - sig_right)], axis=-1).astype(jnp.bfloat16)
    grad_normed = jnp.dot(grad_proj.reshape(N * N, 4 * H), proj_weight.T, preferred_element_type=jnp.float32).reshape(N, N, C)
    scaled_grad = grad_normed * norm_gain
    result = inverse * (scaled_grad - lax.optimization_barrier(jnp.mean(scaled_grad, axis=-1, keepdims=True)) - scaled * lax.optimization_barrier(jnp.mean(scaled_grad * scaled, axis=-1, keepdims=True)))
    return result.astype(jnp.bfloat16)
```

```python
import functools

import jax
import jax.numpy as jnp
from jax import lax
from jax.experimental import pallas as pl
from jax.experimental.pallas import tpu as pltpu
from jax.sharding import PartitionSpec as P

MESH = pl.DeviceIdType.MESH
F32 = jnp.float32
BF16 = jnp.bfloat16


def ring_distance(offset, size):
    return min(offset, size - offset)


def send_order(X, Y, Z):
    offsets = [(a, b, c) for a in range(X) for b in range(Y) for c in range(Z)]
    offsets.remove((0, 0, 0))
    state, shuffled = 12345, []
    while offsets:
        state = (state * 1103515245 + 12345) % (1 << 31)
        shuffled.append(offsets.pop((state >> 8) % len(offsets)))
    paired, seen = [], set()
    for offset in shuffled:
        for one in (offset, ((-offset[0]) % X, (-offset[1]) % Y, (-offset[2]) % Z)):
            if one not in seen:
                seen.add(one)
                paired.append(one)
    def far(o):
        return ring_distance(o[0], X) + ring_distance(o[1], Y) + ring_distance(o[2], Z)

    return sorted(paired, key=lambda o: -far(o))


def kernel(
    RN,
    QN,
    mask_ref,
    pair_hbm,
    grad_hbm,
    gain_ref,
    bias_ref,
    w_ref,
    out_hbm,
    pair_v,
    pair_f,
    grad_v,
    f1,
    f2,
    f3,
    gs,
    ls,
    rs,
    gt,
    lt,
    rt,
    ogr,
    ogl,
    rgr,
    rgl,
    act,
    scaled_s,
    inv_s,
    part,
    out_v,
    wt_s,
    gain_s,
    bias_s,
    load_sem,
    send_sem,
    recv_sem,
    out_sem,
):
    TI, TJ, C = pair_v.shape
    H = gs.shape[0]
    X, Y, Z = 4, QN // 4, RN // 2
    QP = QN // 2
    row, col = lax.axis_index("row"), lax.axis_index("col")
    z, xh = row // 2, row % 2
    qp, core = col // 2, col % 2
    y, xl = qp // 2, qp % 2
    x = xh * 2 + xl
    me = row * QP + qp

    grad_load = pltpu.make_async_copy(grad_hbm, grad_v, load_sem.at[0])
    pair_load = pltpu.make_async_copy(pair_hbm, pair_v, load_sem.at[1])
    grad_load.start()
    pair_load.start()

    peers = []
    for dx, dy, dz in send_order(X, Y, Z):
        px, py, pz = (x + dx) % X, (y + dy) % Y, (z + dz) % Z
        peers.append((pz * 2 + px // 2, py * 2 + px % 2))

    barrier = pltpu.get_barrier_semaphore()
    for prow, pqp in peers:
        pl.semaphore_signal(
            barrier, inc=1, device_id=(prow, pqp * 2 + core), device_id_type=MESH
        )
    pl.semaphore_signal(barrier, inc=1, device_id=(row, qp * 2 + 1 - core), device_id_type=MESH)

    gain_s[...] = jnp.transpose(jnp.broadcast_to(gain_ref[...], (C, C)))
    bias_s[...] = jnp.transpose(jnp.broadcast_to(bias_ref[...], (C, C)))
    wt_s[...] = jnp.transpose(w_ref[...].astype(F32)).astype(BF16)

    def scatter(n, src_of, dst, own_src):
        pltpu.make_async_copy(own_src, dst, recv_sem.at[n]).start()
        for prow, pqp in peers:
            pltpu.make_async_remote_copy(
                src_ref=src_of(prow, pqp),
                dst_ref=dst,
                send_sem=send_sem.at[n],
                recv_sem=recv_sem.at[n],
                device_id=(prow, pqp * 2 + core),
                device_id_type=MESH,
            ).start()

    def wait_for(ref, sem):
        pltpu.make_async_copy(ref, ref, sem).wait()

    grad_load.wait()

    @pl.loop(0, TJ)
    def _(j):
        f1[pl.ds(j * H, H), :] = grad_v[j].astype(F32)

    @pl.loop(0, H)
    def _(c):
        gs[c] = f1[pl.ds(c, TJ, stride=H), :].astype(BF16)

    pl.semaphore_wait(barrier, len(peers) + 1)
    lanes = pl.ds(pl.multiple_of(row * TI, TI), TI)
    by_channel = lambda ref: (lambda prow, pqp: ref.at[prow * QP + pqp])
    scatter(0, by_channel(gs), gt.at[qp, pl.ds(pl.multiple_of(core * TJ, TJ), TJ), lanes], gs.at[me])

    pair_load.wait()

    @pl.loop(0, TI)
    def _(i):
        pair_f[pl.ds(i * TJ, TJ), :] = pair_v[i].astype(F32)

    valid = mask_ref[row, col // 2].astype(F32)
    eye = (
        lax.broadcasted_iota(jnp.int32, (C, C), 0) == lax.broadcasted_iota(jnp.int32, (C, C), 1)
    ).astype(F32).astype(BF16)

    @pl.loop(0, TJ // 2)
    def _(m):
        tokens = jnp.concatenate(
            [pair_f[pl.ds(2 * m + s, TI, stride=TJ), :] for s in (0, 1)], axis=0
        ).astype(BF16)
        values = lax.dot_general(
            eye, tokens, (((1,), (1,)), ((), ())), preferred_element_type=F32
        )
        centred = values - jnp.mean(values, axis=0, keepdims=True)
        variance = jnp.mean(centred * centred, axis=0, keepdims=True)
        inverse = lax.rsqrt(variance + 1e-05)
        scaled = centred * inverse
        gain = jnp.concatenate([gain_s[...], gain_s[...]], axis=1)
        bias = jnp.concatenate([bias_s[...], bias_s[...]], axis=1)
        normed = (scaled * gain + bias).astype(BF16)
        scaled_s[m] = scaled
        inv_s[m] = jnp.broadcast_to(inverse, (8, 2 * TI))
        projected = jnp.dot(wt_s[...], normed, preferred_element_type=F32)
        for side, f in ((0, f2), (1, f3)):
            lin = projected[2 * side * H : (2 * side + 1) * H]
            sig = jax.nn.sigmoid(projected[(2 * side + 1) * H : (2 * side + 2) * H])
            gated = valid * sig
            act[m, pl.ds(2 * side * H, H)] = gated
            act[m, pl.ds((2 * side + 1) * H, H)] = lin * (1.0 - sig)
            activation = gated * lin
            for s in (0, 1):
                f[pl.ds(2 * m + s, H, stride=TJ), :] = activation[:, s * TI : (s + 1) * TI]

    here = (pl.ds(pl.multiple_of(qp * TJ, TJ), TJ), lanes)
    for n, f, s, t in ((1, f2, ls, lt), (2, f3, rs, rt)):

        @pl.loop(0, H)
        def _(c):
            s[c] = f[pl.ds(c * TJ, TJ), :].astype(BF16)

        scatter(n, by_channel(s), t.at[here], s.at[me])

    half = gt.at[:, pl.ds(pl.multiple_of(core * TJ, TJ), TJ), :]
    other = gt.at[:, pl.ds(pl.multiple_of((1 - core) * TJ, TJ), TJ), :]
    wait_for(half, recv_sem.at[0])
    share = pltpu.make_async_remote_copy(
        src_ref=half,
        dst_ref=half,
        send_sem=send_sem.at[5],
        recv_sem=recv_sem.at[5],
        device_id=(row, qp * 2 + 1 - core),
        device_id_type=MESH,
    )
    share.start()
    wait_for(other, recv_sem.at[5])

    def block_of(ref):
        return lambda prow, pqp: ref.at[
            pl.ds(pl.multiple_of(pqp * TJ, TJ), TJ), pl.ds(pl.multiple_of(prow * TI, TI), TI)
        ]

    wait_for(lt, recv_sem.at[1])

    @pl.loop(0, RN // 2)
    def _(n):
        g = gt[pl.ds(n * 2, 2)].reshape(2 * TI, RN * TI)
        ogr[:, pl.ds(pl.multiple_of(n * 2 * TI, 2 * TI), 2 * TI)] = lax.dot_general(
            lt[...], g, (((1,), (1,)), ((), ())), preferred_element_type=F32
        ).astype(BF16)

    scatter(3, block_of(ogr), rgr.at[me], block_of(ogr)(row, qp))

    wait_for(rt, recv_sem.at[2])

    @pl.loop(0, RN // 2)
    def _(n):
        cols = pl.ds(pl.multiple_of(n * 2 * TI, 2 * TI), 2 * TI)
        g = gt[:, :, cols].reshape(RN * TI, 2 * TI)
        ogl[:, cols] = jnp.dot(rt[...], g, preferred_element_type=F32).astype(BF16)

    scatter(4, block_of(ogl), rgl.at[me], block_of(ogl)(row, qp))

    def grad_proj(f, m, side):
        g = jnp.concatenate([f[pl.ds(2 * m + s, H, stride=TJ), :] for s in (0, 1)], axis=1)
        lin = g * act[m, pl.ds(2 * side * H, H)]
        gate = lin * act[m, pl.ds((2 * side + 1) * H, H)]
        return jnp.concatenate([lin, gate], axis=0).astype(BF16)

    wait_for(rgr, recv_sem.at[3])

    @pl.loop(0, H)
    def _(c):
        f3[pl.ds(c * TJ, TJ), :] = rgr[c].astype(F32)

    @pl.loop(0, TJ // 2)
    def _(m):
        part[m] = jnp.dot(
            w_ref[:, 2 * H : 4 * H], grad_proj(f3, m, 1), preferred_element_type=F32
        )

    wait_for(rgl, recv_sem.at[4])

    @pl.loop(0, H)
    def _(c):
        f2[pl.ds(c * TJ, TJ), :] = rgl[c].astype(F32)

    @pl.loop(0, TJ // 2)
    def _(m):
        grad_normed = part[m] + jnp.dot(
            w_ref[:, 0 : 2 * H], grad_proj(f2, m, 0), preferred_element_type=F32
        )
        gain = jnp.concatenate([gain_s[...], gain_s[...]], axis=1)
        scaled = scaled_s[m]
        g = grad_normed * gain
        result = inv_s[m, 0:1] * (
            g
            - jnp.mean(g, axis=0, keepdims=True)
            - scaled * jnp.mean(g * scaled, axis=0, keepdims=True)
        )
        result = result.astype(BF16)
        for s in (0, 1):
            out_v[2 * m + s] = result[:, s * TI : (s + 1) * TI]

    store = pltpu.make_async_copy(out_v, out_hbm, out_sem)
    store.start()

    for n, buf in enumerate((gs, ls, rs, rgr, rgl)):
        if len(peers):
            wait_for(buf.at[pl.ds(0, len(peers))], send_sem.at[n])
    wait_for(half, send_sem.at[5])
    store.wait()


def shards(RN, QN, pair, grad_x, norm_gain, norm_bias, proj_weight, tile_mask):
    TI, TJ, C = pair.shape
    H = grad_x.shape[2]
    QP = QN // 2
    N = RN * TI
    vmem = lambda *shape: pltpu.VMEM(shape[:-1], shape[-1])
    any_space = pl.BlockSpec(memory_space=pl.ANY)
    in_vmem = pl.BlockSpec(memory_space=pltpu.VMEM)
    out = pl.pallas_call(
        functools.partial(kernel, RN, QN),
        out_shape=jax.ShapeDtypeStruct((TJ, C, TI), BF16),
        in_specs=[
            pl.BlockSpec(memory_space=pltpu.SMEM),
            any_space,
            any_space,
            in_vmem,
            in_vmem,
            in_vmem,
        ],
        out_specs=any_space,
        scratch_shapes=[
            vmem(TI, TJ, C, BF16),
            vmem(TI * TJ, C, F32),
            vmem(TJ, H, TI, BF16),
            vmem(TJ * H, TI, F32),
            vmem(TJ * H, TI, F32),
            vmem(TJ * H, TI, F32),
            vmem(H, TJ, TI, BF16),
            vmem(H, TJ, TI, BF16),
            vmem(H, TJ, TI, BF16),
            vmem(QP, 2 * TJ, N, BF16),
            vmem(QP * TJ, N, BF16),
            vmem(QP * TJ, N, BF16),
            vmem(QP * TJ, N, BF16),
            vmem(QP * TJ, N, BF16),
            vmem(H, TJ, TI, BF16),
            vmem(H, TJ, TI, BF16),
            vmem(TJ // 2, 4 * H, 2 * TI, F32),
            vmem(TJ // 2, C, 2 * TI, F32),
            vmem(TJ // 2, 8, 2 * TI, F32),
            vmem(TJ // 2, C, 2 * TI, F32),
            vmem(TJ, C, TI, BF16),
            vmem(4 * H, C, BF16),
            vmem(C, C, F32),
            vmem(C, C, F32),
            pltpu.SemaphoreType.DMA((2,)),
            pltpu.SemaphoreType.DMA((6,)),
            pltpu.SemaphoreType.DMA((6,)),
            pltpu.SemaphoreType.DMA(()),
        ],
        compiler_params=pltpu.CompilerParams(
            collective_id=0, has_side_effects=True, vmem_limit_bytes=60 << 20
        ),
    )(
        tile_mask,
        pair,
        jnp.transpose(grad_x, (1, 2, 0)),
        norm_gain.reshape(1, C),
        norm_bias.reshape(1, C),
        proj_weight,
    )
    return jnp.transpose(out, (2, 0, 1))


def solution(mesh):
    placed = (P("row", "col", None), P("row", "col", None), P(), P(), P(), P())
    body = functools.partial(shards, mesh.shape["row"], mesh.shape["col"])
    return jax.shard_map(
        body, mesh=mesh, in_specs=placed, out_specs=P("row", "col", None), check_vma=False
    )
```

```python
import functools

import jax
import jax.numpy as jnp
from jax import lax
from jax.experimental import pallas as pl
from jax.experimental.pallas import tpu as pltpu
from jax.sharding import PartitionSpec as P

MESH = pl.DeviceIdType.MESH
F32 = jnp.float32
BF16 = jnp.bfloat16


def ring_distance(offset, size):
    return min(offset, size - offset)


def send_order(X, Y, Z):
    offsets = [(a, b, c) for a in range(X) for b in range(Y) for c in range(Z)]
    offsets.remove((0, 0, 0))
    state, shuffled = 12345, []
    while offsets:
        state = (state * 1103515245 + 12345) % (1 << 31)
        shuffled.append(offsets.pop((state >> 8) % len(offsets)))
    paired, seen = [], set()
    for offset in shuffled:
        for one in (offset, ((-offset[0]) % X, (-offset[1]) % Y, (-offset[2]) % Z)):
            if one not in seen:
                seen.add(one)
                paired.append(one)
    def far(o):
        return ring_distance(o[0], X) + ring_distance(o[1], Y) + ring_distance(o[2], Z)

    return sorted(paired, key=lambda o: -far(o))


def kernel(
    RN,
    QN,
    mask_ref,
    pair_hbm,
    grad_hbm,
    gain_ref,
    bias_ref,
    w_ref,
    out_hbm,
    pair_v,
    pair_f,
    grad_v,
    f1,
    f2,
    f3,
    gs,
    ls,
    rs,
    gt,
    lt,
    rt,
    ogr,
    ogl,
    rgr,
    rgl,
    act,
    scaled_s,
    inv_s,
    part,
    normed_s,
    out_v,
    wt_s,
    gain_s,
    bias_s,
    load_sem,
    send_sem,
    recv_sem,
    out_sem,
):
    TI, TJ, C = pair_v.shape
    H = gs.shape[0]
    X, Y, Z = 4, QN // 4, RN // 2
    QP = QN // 2
    pitch = f1.shape[0] // TJ
    row, col = lax.axis_index("row"), lax.axis_index("col")
    z, xh = row // 2, row % 2
    qp, core = col // 2, col % 2
    y, xl = qp // 2, qp % 2
    x = xh * 2 + xl
    me = row * QP + qp

    grad_load = pltpu.make_async_copy(grad_hbm, grad_v, load_sem.at[0])
    pair_load = pltpu.make_async_copy(pair_hbm, pair_v, load_sem.at[1])
    grad_load.start()
    pair_load.start()

    peers = []
    for dx, dy, dz in send_order(X, Y, Z):
        px, py, pz = (x + dx) % X, (y + dy) % Y, (z + dz) % Z
        peers.append((pz * 2 + px // 2, py * 2 + px % 2))

    barrier = pltpu.get_barrier_semaphore()
    for prow, pqp in peers:
        pl.semaphore_signal(
            barrier, inc=1, device_id=(prow, pqp * 2 + core), device_id_type=MESH
        )
    pl.semaphore_signal(barrier, inc=1, device_id=(row, qp * 2 + 1 - core), device_id_type=MESH)

    gain_s[...] = jnp.transpose(jnp.broadcast_to(gain_ref[...], (C, C)))
    bias_s[...] = jnp.transpose(jnp.broadcast_to(bias_ref[...], (C, C)))
    wt_s[...] = jnp.transpose(w_ref[...].astype(F32)).astype(BF16)

    def scatter(n, src_of, dst, own_src):
        pltpu.make_async_copy(own_src, dst, recv_sem.at[n]).start()
        for prow, pqp in peers:
            pltpu.make_async_remote_copy(
                src_ref=src_of(prow, pqp),
                dst_ref=dst,
                send_sem=send_sem.at[n],
                recv_sem=recv_sem.at[n],
                device_id=(prow, pqp * 2 + core),
                device_id_type=MESH,
            ).start()

    def wait_for(ref, sem):
        pltpu.make_async_copy(ref, ref, sem).wait()

    grad_load.wait()

    @pl.loop(0, TJ, unroll=4)
    def _(j):
        f1[pl.ds(j * pitch, H), :] = grad_v[j].astype(F32)

    @pl.loop(0, H, unroll=4)
    def _(c):
        gs[c] = f1[pl.ds(c, TJ, stride=pitch), :].astype(BF16)

    pl.semaphore_wait(barrier, len(peers) + 1)
    lanes = pl.ds(pl.multiple_of(row * TI, TI), TI)
    by_channel = lambda ref: (lambda prow, pqp: ref.at[prow * QP + pqp])
    scatter(0, by_channel(gs), gt.at[qp, pl.ds(pl.multiple_of(core * TJ, TJ), TJ), lanes], gs.at[me])

    pair_load.wait()

    @pl.loop(0, TI, unroll=4)
    def _(i):
        pair_f[pl.ds(i * pitch, TJ), :] = pair_v[i].astype(F32)

    valid = mask_ref[row, col // 2].astype(F32)
    eye = (
        lax.broadcasted_iota(jnp.int32, (C, C), 0) == lax.broadcasted_iota(jnp.int32, (C, C), 1)
    ).astype(F32).astype(BF16)

    def activate(m, normed, side, f):
        projected = jnp.dot(
            wt_s[pl.ds(2 * side * H, 2 * H), :], normed, preferred_element_type=F32
        )
        lin = projected[0:H]
        sig = jax.nn.sigmoid(projected[H : 2 * H])
        gated = valid * sig
        act[m, pl.ds(2 * side * H, H)] = gated
        act[m, pl.ds((2 * side + 1) * H, H)] = lin * (1.0 - sig)
        activation = gated * lin
        for s in (0, 1):
            f[pl.ds(2 * m + s, H, stride=pitch), :] = activation[:, s * TI : (s + 1) * TI]

    here = (pl.ds(pl.multiple_of(qp * TJ, TJ), TJ), lanes)

    def send_activation(n, f, s, t):
        @pl.loop(0, H, unroll=4)
        def _(c):
            s[c] = f[pl.ds(c * pitch, TJ), :].astype(BF16)

        scatter(n, by_channel(s), t.at[here], s.at[me])

    @pl.loop(0, TJ // 2, unroll=2)
    def _(m):
        tokens = jnp.concatenate(
            [pair_f[pl.ds(2 * m + s, TI, stride=pitch), :] for s in (0, 1)], axis=0
        ).astype(BF16)
        values = lax.dot_general(
            eye, tokens, (((1,), (1,)), ((), ())), preferred_element_type=F32
        )
        centred = values - jnp.mean(values, axis=0, keepdims=True)
        variance = jnp.mean(centred * centred, axis=0, keepdims=True)
        inverse = lax.rsqrt(variance + 1e-05)
        scaled = centred * inverse
        gain = jnp.concatenate([gain_s[...], gain_s[...]], axis=1)
        bias = jnp.concatenate([bias_s[...], bias_s[...]], axis=1)
        normed = (scaled * gain + bias).astype(BF16)
        scaled_s[m] = scaled
        inv_s[m] = jnp.broadcast_to(inverse, (8, 2 * TI))
        normed_s[m] = normed
        activate(m, normed, 0, f2)

    send_activation(1, f2, ls, lt)

    @pl.loop(0, TJ // 2, unroll=2)
    def _(m):
        activate(m, normed_s[m], 1, f3)

    send_activation(2, f3, rs, rt)

    half = gt.at[:, pl.ds(pl.multiple_of(core * TJ, TJ), TJ), :]
    other = gt.at[:, pl.ds(pl.multiple_of((1 - core) * TJ, TJ), TJ), :]
    wait_for(half, recv_sem.at[0])
    share = pltpu.make_async_remote_copy(
        src_ref=half,
        dst_ref=half,
        send_sem=send_sem.at[6],
        recv_sem=recv_sem.at[6],
        device_id=(row, qp * 2 + 1 - core),
        device_id_type=MESH,
    )
    share.start()
    wait_for(other, recv_sem.at[6])

    def block_of(ref):
        return lambda prow, pqp: ref.at[
            pl.ds(pl.multiple_of(pqp * TJ, TJ), TJ), pl.ds(pl.multiple_of(prow * TI, TI), TI)
        ]

    wait_for(lt, recv_sem.at[1])

    @pl.loop(0, RN // 2)
    def _(n):
        g = gt[pl.ds(n * 2, 2)].reshape(2 * TI, RN * TI)
        ogr[:, pl.ds(pl.multiple_of(n * 2 * TI, 2 * TI), 2 * TI)] = lax.dot_general(
            lt[...], g, (((1,), (1,)), ((), ())), preferred_element_type=F32
        ).astype(BF16)

    scatter(3, block_of(ogr), rgr.at[me], block_of(ogr)(row, qp))

    wait_for(rt, recv_sem.at[2])

    @pl.loop(0, RN // 2)
    def _(n):
        cols = pl.ds(pl.multiple_of(n * 2 * TI, 2 * TI), 2 * TI)
        g = gt[:, :, cols].reshape(RN * TI, 2 * TI)
        ogl[:, cols] = jnp.dot(rt[...], g, preferred_element_type=F32).astype(BF16)

    HK = TJ // 2

    def part_of(ref, half_k):
        return lambda prow, pqp: ref.at[
            pl.ds(pl.multiple_of(pqp * TJ + half_k * HK, HK), HK),
            pl.ds(pl.multiple_of(prow * TI, TI), TI),
        ]

    for hk in (0, 1):
        scatter(4 + hk, part_of(ogl, hk), rgl.at[me, pl.ds(hk * HK, HK)], part_of(ogl, hk)(row, qp))

    def grad_proj(f, m, side):
        g = jnp.concatenate([f[pl.ds(2 * m + s, H, stride=pitch), :] for s in (0, 1)], axis=1)
        lin = g * act[m, pl.ds(2 * side * H, H)]
        gate = lin * act[m, pl.ds((2 * side + 1) * H, H)]
        return jnp.concatenate([lin, gate], axis=0).astype(BF16)

    wait_for(rgr, recv_sem.at[3])

    @pl.loop(0, H, unroll=4)
    def _(c):
        f3[pl.ds(c * pitch, TJ), :] = rgr[c].astype(F32)

    @pl.loop(0, TJ // 2, unroll=2)
    def _(m):
        part[m] = jnp.dot(
            w_ref[:, 2 * H : 4 * H], grad_proj(f3, m, 1), preferred_element_type=F32
        )

    for hk in (0, 1):
        wait_for(rgl.at[:, pl.ds(hk * HK, HK)], recv_sem.at[4 + hk])

        @pl.loop(0, H, unroll=4)
        def _(c):
            f2[pl.ds(c * pitch + hk * HK, HK), :] = rgl[c, pl.ds(hk * HK, HK)].astype(F32)

        @pl.loop(hk * HK // 2, (hk + 1) * HK // 2, unroll=2)
        def _(m):
            grad_normed = part[m] + jnp.dot(
                w_ref[:, 0 : 2 * H], grad_proj(f2, m, 0), preferred_element_type=F32
            )
            gain = jnp.concatenate([gain_s[...], gain_s[...]], axis=1)
            scaled = scaled_s[m]
            g = grad_normed * gain
            result = inv_s[m, 0:1] * (
                g
                - jnp.mean(g, axis=0, keepdims=True)
                - scaled * jnp.mean(g * scaled, axis=0, keepdims=True)
            )
            result = result.astype(BF16)
            for s in (0, 1):
                out_v[2 * m + s] = result[:, s * TI : (s + 1) * TI]

        rows = pl.ds(hk * HK, HK)
        pltpu.make_async_copy(out_v.at[rows], out_hbm.at[rows], out_sem.at[hk]).start()

    for n, buf in enumerate((gs, ls, rs, rgr)):
        wait_for(buf.at[pl.ds(0, len(peers))], send_sem.at[n])
    for hk in (0, 1):
        rows = pl.ds(hk * HK, HK)
        wait_for(rgl.at[pl.ds(0, len(peers)), rows], send_sem.at[4 + hk])
        pltpu.make_async_copy(out_v.at[rows], out_hbm.at[rows], out_sem.at[hk]).wait()
    wait_for(half, send_sem.at[6])


def shards(RN, QN, pair, grad_x, norm_gain, norm_bias, proj_weight, tile_mask):
    TI, TJ, C = pair.shape
    H = grad_x.shape[2]
    QP = QN // 2
    N = RN * TI
    pitch = TJ + 8
    vmem = lambda *shape: pltpu.VMEM(shape[:-1], shape[-1])
    any_space = pl.BlockSpec(memory_space=pl.ANY)
    in_vmem = pl.BlockSpec(memory_space=pltpu.VMEM)
    out = pl.pallas_call(
        functools.partial(kernel, RN, QN),
        out_shape=jax.ShapeDtypeStruct((TJ, C, TI), BF16),
        in_specs=[
            pl.BlockSpec(memory_space=pltpu.SMEM),
            any_space,
            any_space,
            in_vmem,
            in_vmem,
            in_vmem,
        ],
        out_specs=any_space,
        scratch_shapes=[
            vmem(TI, TJ, C, BF16),
            vmem(TI * pitch, C, F32),
            vmem(TJ, H, TI, BF16),
            vmem(TJ * pitch, TI, F32),
            vmem(TJ * pitch, TI, F32),
            vmem(TJ * pitch, TI, F32),
            vmem(H, TJ, TI, BF16),
            vmem(H, TJ, TI, BF16),
            vmem(H, TJ, TI, BF16),
            vmem(QP, 2 * TJ, N, BF16),
            vmem(QP * TJ, N, BF16),
            vmem(QP * TJ, N, BF16),
            vmem(QP * TJ, N, BF16),
            vmem(QP * TJ, N, BF16),
            vmem(H, TJ, TI, BF16),
            vmem(H, TJ, TI, BF16),
            vmem(TJ // 2, 4 * H, 2 * TI, F32),
            vmem(TJ // 2, C, 2 * TI, F32),
            vmem(TJ // 2, 8, 2 * TI, F32),
            vmem(TJ // 2, C, 2 * TI, F32),
            vmem(TJ // 2, C, 2 * TI, BF16),
            vmem(TJ, C, TI, BF16),
            vmem(4 * H, C, BF16),
            vmem(C, C, F32),
            vmem(C, C, F32),
            pltpu.SemaphoreType.DMA((2,)),
            pltpu.SemaphoreType.DMA((7,)),
            pltpu.SemaphoreType.DMA((7,)),
            pltpu.SemaphoreType.DMA((2,)),
        ],
        compiler_params=pltpu.CompilerParams(
            collective_id=0, has_side_effects=True, vmem_limit_bytes=60 << 20
        ),
    )(
        tile_mask,
        pair,
        jnp.transpose(grad_x, (1, 2, 0)),
        norm_gain.reshape(1, C),
        norm_bias.reshape(1, C),
        proj_weight,
    )
    return jnp.transpose(out, (2, 0, 1))


def solution(mesh):
    placed = (P("row", "col", None), P("row", "col", None), P(), P(), P(), P())
    body = functools.partial(shards, mesh.shape["row"], mesh.shape["col"])
    return jax.shard_map(
        body, mesh=mesh, in_specs=placed, out_specs=P("row", "col", None), check_vma=False
    )
```

```python
import functools

import jax
import jax.numpy as jnp
from jax import lax
from jax.experimental import pallas as pl
from jax.experimental.pallas import tpu as pltpu
from jax.sharding import PartitionSpec as P

MESH = pl.DeviceIdType.MESH
F32 = jnp.float32
BF16 = jnp.bfloat16


def ring_distance(offset, size):
    return min(offset, size - offset)


def send_order(X, Y, Z):
    offsets = [(a, b, c) for a in range(X) for b in range(Y) for c in range(Z)]
    offsets.remove((0, 0, 0))
    state, shuffled = 12345, []
    while offsets:
        state = (state * 1103515245 + 12345) % (1 << 31)
        shuffled.append(offsets.pop((state >> 8) % len(offsets)))
    paired, seen = [], set()
    for offset in shuffled:
        for one in (offset, ((-offset[0]) % X, (-offset[1]) % Y, (-offset[2]) % Z)):
            if one not in seen:
                seen.add(one)
                paired.append(one)
    def far(o):
        return ring_distance(o[0], X) + ring_distance(o[1], Y) + ring_distance(o[2], Z)

    return sorted(paired, key=lambda o: -far(o))


def kernel(
    RN,
    QN,
    mask_ref,
    pair_hbm,
    grad_hbm,
    gain_ref,
    bias_ref,
    w_ref,
    out_ref,
    pair_v,
    pair_f,
    grad_v,
    f1,
    f2,
    f3,
    gs,
    ls,
    rs,
    gt,
    lt,
    rt,
    ogr,
    ogl,
    rgr,
    rgl,
    act,
    scaled_s,
    inv_s,
    part,
    normed_s,
    wt_s,
    gain_s,
    bias_s,
    load_sem,
    send_sem,
    recv_sem,
):
    TI, TJ, C = pair_v.shape
    H = gs.shape[0]
    X, Y, Z = 4, QN // 4, RN // 2
    QP = QN // 2
    pitch = f1.shape[0] // TJ
    row, col = lax.axis_index("row"), lax.axis_index("col")
    z, xh = row // 2, row % 2
    qp, core = col // 2, col % 2
    y, xl = qp // 2, qp % 2
    x = xh * 2 + xl
    me = row * QP + qp

    grad_load = pltpu.make_async_copy(grad_hbm, grad_v, load_sem.at[0])
    pair_load = pltpu.make_async_copy(pair_hbm, pair_v, load_sem.at[1])
    grad_load.start()
    pair_load.start()

    peers = []
    for dx, dy, dz in send_order(X, Y, Z):
        px, py, pz = (x + dx) % X, (y + dy) % Y, (z + dz) % Z
        peers.append((pz * 2 + px // 2, py * 2 + px % 2))

    barrier = pltpu.get_barrier_semaphore()
    for prow, pqp in peers:
        pl.semaphore_signal(
            barrier, inc=1, device_id=(prow, pqp * 2 + core), device_id_type=MESH
        )
    pl.semaphore_signal(barrier, inc=1, device_id=(row, qp * 2 + 1 - core), device_id_type=MESH)

    gain_s[...] = jnp.transpose(jnp.broadcast_to(gain_ref[...], (C, C)))
    bias_s[...] = jnp.transpose(jnp.broadcast_to(bias_ref[...], (C, C)))
    wt_s[...] = jnp.transpose(w_ref[...].astype(F32)).astype(BF16)

    def scatter(n, src_of, dst, own_src):
        pltpu.make_async_copy(own_src, dst, recv_sem.at[n]).start()
        for prow, pqp in peers:
            pltpu.make_async_remote_copy(
                src_ref=src_of(prow, pqp),
                dst_ref=dst,
                send_sem=send_sem.at[n],
                recv_sem=recv_sem.at[n],
                device_id=(prow, pqp * 2 + core),
                device_id_type=MESH,
            ).start()

    def wait_for(ref, sem):
        pltpu.make_async_copy(ref, ref, sem).wait()

    grad_load.wait()

    @pl.loop(0, TJ, unroll=4)
    def _(j):
        f1[pl.ds(j * pitch, H), :] = grad_v[j].astype(F32)

    @pl.loop(0, H, unroll=4)
    def _(c):
        gs[c] = f1[pl.ds(c, TJ, stride=pitch), :].astype(BF16)

    pl.semaphore_wait(barrier, len(peers) + 1)
    lanes = pl.ds(pl.multiple_of(row * TI, TI), TI)
    by_channel = lambda ref: (lambda prow, pqp: ref.at[prow * QP + pqp])
    scatter(0, by_channel(gs), gt.at[qp, pl.ds(pl.multiple_of(core * TJ, TJ), TJ), lanes], gs.at[me])

    pair_load.wait()

    @pl.loop(0, TI, unroll=4)
    def _(i):
        pair_f[pl.ds(i * pitch, TJ), :] = pair_v[i].astype(F32)

    valid = mask_ref[row, col // 2].astype(F32)
    eye = (
        lax.broadcasted_iota(jnp.int32, (C, C), 0) == lax.broadcasted_iota(jnp.int32, (C, C), 1)
    ).astype(F32).astype(BF16)

    def activate(m, normed, side, f):
        projected = jnp.dot(
            wt_s[pl.ds(2 * side * H, 2 * H), :], normed, preferred_element_type=F32
        )
        lin = projected[0:H]
        sig = jax.nn.sigmoid(projected[H : 2 * H])
        gated = valid * sig
        act[m, pl.ds(2 * side * H, H)] = gated
        act[m, pl.ds((2 * side + 1) * H, H)] = lin * (1.0 - sig)
        activation = gated * lin
        for s in (0, 1):
            f[pl.ds(2 * m + s, H, stride=pitch), :] = activation[:, s * TI : (s + 1) * TI]

    here = (pl.ds(pl.multiple_of(qp * TJ, TJ), TJ), lanes)

    def send_activation(n, f, s, t):
        @pl.loop(0, H, unroll=4)
        def _(c):
            s[c] = f[pl.ds(c * pitch, TJ), :].astype(BF16)

        scatter(n, by_channel(s), t.at[here], s.at[me])

    @pl.loop(0, TJ // 2, unroll=2)
    def _(m):
        tokens = jnp.concatenate(
            [pair_f[pl.ds(2 * m + s, TI, stride=pitch), :] for s in (0, 1)], axis=0
        ).astype(BF16)
        values = lax.dot_general(
            eye, tokens, (((1,), (1,)), ((), ())), preferred_element_type=F32
        )
        centred = values - jnp.mean(values, axis=0, keepdims=True)
        variance = jnp.mean(centred * centred, axis=0, keepdims=True)
        inverse = lax.rsqrt(variance + 1e-05)
        scaled = centred * inverse
        gain = jnp.concatenate([gain_s[...], gain_s[...]], axis=1)
        bias = jnp.concatenate([bias_s[...], bias_s[...]], axis=1)
        normed = (scaled * gain + bias).astype(BF16)
        scaled_s[m] = scaled
        inv_s[m] = jnp.broadcast_to(inverse, (8, 2 * TI))
        normed_s[m] = normed
        activate(m, normed, 0, f2)

    send_activation(1, f2, ls, lt)

    @pl.loop(0, TJ // 2, unroll=2)
    def _(m):
        activate(m, normed_s[m], 1, f3)

    send_activation(2, f3, rs, rt)

    half = gt.at[:, pl.ds(pl.multiple_of(core * TJ, TJ), TJ), :]
    other = gt.at[:, pl.ds(pl.multiple_of((1 - core) * TJ, TJ), TJ), :]
    wait_for(half, recv_sem.at[0])
    share = pltpu.make_async_remote_copy(
        src_ref=half,
        dst_ref=half,
        send_sem=send_sem.at[6],
        recv_sem=recv_sem.at[6],
        device_id=(row, qp * 2 + 1 - core),
        device_id_type=MESH,
    )
    share.start()
    wait_for(other, recv_sem.at[6])

    def block_of(ref):
        return lambda prow, pqp: ref.at[
            pl.ds(pl.multiple_of(pqp * TJ, TJ), TJ), pl.ds(pl.multiple_of(prow * TI, TI), TI)
        ]

    wait_for(lt, recv_sem.at[1])

    @pl.loop(0, RN // 2)
    def _(n):
        g = gt[pl.ds(n * 2, 2)].reshape(2 * TI, RN * TI)
        ogr[:, pl.ds(pl.multiple_of(n * 2 * TI, 2 * TI), 2 * TI)] = lax.dot_general(
            lt[...], g, (((1,), (1,)), ((), ())), preferred_element_type=F32
        ).astype(BF16)

    scatter(3, block_of(ogr), rgr.at[me], block_of(ogr)(row, qp))

    wait_for(rt, recv_sem.at[2])

    @pl.loop(0, RN // 2)
    def _(n):
        cols = pl.ds(pl.multiple_of(n * 2 * TI, 2 * TI), 2 * TI)
        g = gt[:, :, cols].reshape(RN * TI, 2 * TI)
        ogl[:, cols] = jnp.dot(rt[...], g, preferred_element_type=F32).astype(BF16)

    HK = TJ // 2

    def part_of(ref, half_k):
        return lambda prow, pqp: ref.at[
            pl.ds(pl.multiple_of(pqp * TJ + half_k * HK, HK), HK),
            pl.ds(pl.multiple_of(prow * TI, TI), TI),
        ]

    for hk in (0, 1):
        scatter(4 + hk, part_of(ogl, hk), rgl.at[me, pl.ds(hk * HK, HK)], part_of(ogl, hk)(row, qp))

    def grad_proj(f, m, side):
        g = jnp.concatenate([f[pl.ds(2 * m + s, H, stride=pitch), :] for s in (0, 1)], axis=1)
        lin = g * act[m, pl.ds(2 * side * H, H)]
        gate = lin * act[m, pl.ds((2 * side + 1) * H, H)]
        return jnp.concatenate([lin, gate], axis=0).astype(BF16)

    wait_for(rgr, recv_sem.at[3])

    @pl.loop(0, H, unroll=4)
    def _(c):
        f3[pl.ds(c * pitch, TJ), :] = rgr[c].astype(F32)

    @pl.loop(0, TJ // 2, unroll=2)
    def _(m):
        part[m] = jnp.dot(
            w_ref[:, 2 * H : 4 * H], grad_proj(f3, m, 1), preferred_element_type=F32
        )

    for hk in (0, 1):
        wait_for(rgl.at[:, pl.ds(hk * HK, HK)], recv_sem.at[4 + hk])

        @pl.loop(0, H, unroll=4)
        def _(c):
            f2[pl.ds(c * pitch + hk * HK, HK), :] = rgl[c, pl.ds(hk * HK, HK)].astype(F32)

        @pl.loop(hk * HK // 2, (hk + 1) * HK // 2, unroll=2)
        def _(m):
            grad_normed = part[m] + jnp.dot(
                w_ref[:, 0 : 2 * H], grad_proj(f2, m, 0), preferred_element_type=F32
            )
            gain = jnp.concatenate([gain_s[...], gain_s[...]], axis=1)
            scaled = scaled_s[m]
            g = grad_normed * gain
            result = inv_s[m, 0:1] * (
                g
                - jnp.mean(g, axis=0, keepdims=True)
                - scaled * jnp.mean(g * scaled, axis=0, keepdims=True)
            )
            for s in (0, 1):
                pair_f[pl.ds(2 * m + s, TI, stride=pitch), :] = jnp.transpose(
                    result[:, s * TI : (s + 1) * TI]
                )

        @pl.loop(0, TI, unroll=4)
        def _(i):
            out_ref[i, pl.ds(hk * HK, HK)] = pair_f[pl.ds(i * pitch + hk * HK, HK), :].astype(BF16)

    for n, buf in enumerate((gs, ls, rs, rgr)):
        wait_for(buf.at[pl.ds(0, len(peers))], send_sem.at[n])
    for hk in (0, 1):
        rows = pl.ds(hk * HK, HK)
        wait_for(rgl.at[pl.ds(0, len(peers)), rows], send_sem.at[4 + hk])
    wait_for(half, send_sem.at[6])


def shards(RN, QN, pair, grad_x, norm_gain, norm_bias, proj_weight, tile_mask):
    TI, TJ, C = pair.shape
    H = grad_x.shape[2]
    QP = QN // 2
    N = RN * TI
    pitch = TJ + 8
    vmem = lambda *shape: pltpu.VMEM(shape[:-1], shape[-1])
    any_space = pl.BlockSpec(memory_space=pl.ANY)
    in_vmem = pl.BlockSpec(memory_space=pltpu.VMEM)
    out = pl.pallas_call(
        functools.partial(kernel, RN, QN),
        out_shape=pltpu.VMEM((TI, TJ, C), BF16),
        in_specs=[
            pl.BlockSpec(memory_space=pltpu.SMEM),
            any_space,
            any_space,
            in_vmem,
            in_vmem,
            in_vmem,
        ],
        out_specs=in_vmem,
        scratch_shapes=[
            vmem(TI, TJ, C, BF16),
            vmem(TI * pitch, C, F32),
            vmem(TJ, H, TI, BF16),
            vmem(TJ * pitch, TI, F32),
            vmem(TJ * pitch, TI, F32),
            vmem(TJ * pitch, TI, F32),
            vmem(H, TJ, TI, BF16),
            vmem(H, TJ, TI, BF16),
            vmem(H, TJ, TI, BF16),
            vmem(QP, 2 * TJ, N, BF16),
            vmem(QP * TJ, N, BF16),
            vmem(QP * TJ, N, BF16),
            vmem(QP * TJ, N, BF16),
            vmem(QP * TJ, N, BF16),
            vmem(H, TJ, TI, BF16),
            vmem(H, TJ, TI, BF16),
            vmem(TJ // 2, 4 * H, 2 * TI, F32),
            vmem(TJ // 2, C, 2 * TI, F32),
            vmem(TJ // 2, 8, 2 * TI, F32),
            vmem(TJ // 2, C, 2 * TI, F32),
            vmem(TJ // 2, C, 2 * TI, BF16),
            vmem(4 * H, C, BF16),
            vmem(C, C, F32),
            vmem(C, C, F32),
            pltpu.SemaphoreType.DMA((2,)),
            pltpu.SemaphoreType.DMA((7,)),
            pltpu.SemaphoreType.DMA((7,)),
        ],
        compiler_params=pltpu.CompilerParams(
            collective_id=0, has_side_effects=True, vmem_limit_bytes=60 << 20
        ),
    )(
        tile_mask,
        pair,
        jnp.transpose(grad_x, (1, 2, 0)),
        norm_gain.reshape(1, C),
        norm_bias.reshape(1, C),
        proj_weight,
    )
    return out


def solution(mesh):
    placed = (P("row", "col", None), P("row", "col", None), P(), P(), P(), P())
    body = functools.partial(shards, mesh.shape["row"], mesh.shape["col"])
    return jax.shard_map(
        body, mesh=mesh, in_specs=placed, out_specs=P("row", "col", None), check_vma=False
    )
```

```python
import functools

import jax
import jax.numpy as jnp
from jax import lax
from jax.experimental import pallas as pl
from jax.experimental.pallas import tpu as pltpu
from jax.sharding import PartitionSpec as P

MESH = pl.DeviceIdType.MESH
F32 = jnp.float32
BF16 = jnp.bfloat16


SEND_ORDER = (
    42, 48, 58, 16, 46, 4, 38, 1, 41, 12, 26, 3, 43, 17, 57, 51,
    10, 2, 47, 8, 22, 7, 62, 49, 39, 32, 27, 5, 37, 20, 25, 15,
    59, 60, 30, 19, 34, 13, 54, 28, 45, 52, 40, 23, 53, 61, 36, 50,
    33, 55, 9, 11, 56, 24, 44, 31, 63, 35, 21, 14, 29, 18, 6,
)


def send_order(X, Y, Z):
    assert (X, Y, Z) == (4, 4, 4)
    return [(code // 16, code // 4 % 4, code % 4) for code in SEND_ORDER]


def kernel(
    RN,
    QN,
    mask_hbm,
    pair_hbm,
    grad_hbm,
    gain_hbm,
    bias_hbm,
    w_hbm,
    out_ref,
    mask_ref,
    gain_ref,
    bias_ref,
    w_ref,
    pair_v,
    pair_f,
    grad_v,
    f1,
    f2,
    f3,
    gs,
    ls,
    rs,
    gt,
    lt,
    rt,
    ogr,
    ogl,
    rgr,
    rgl,
    act,
    scaled_s,
    inv_s,
    part,
    normed_s,
    wt_s,
    gain_s,
    bias_s,
    load_sem,
    send_sem,
    recv_sem,
):
    TI, TJ, C = pair_v.shape
    H = gs.shape[0]
    X, Y, Z = 4, QN // 4, RN // 2
    QP = QN // 2
    pitch = f1.shape[0] // TJ
    row, col = lax.axis_index("row"), lax.axis_index("col")
    z, xh = row // 2, row % 2
    qp, core = col // 2, col % 2
    y, xl = qp // 2, qp % 2
    x = xh * 2 + xl
    me = row * QP + qp

    grad_load = pltpu.make_async_copy(grad_hbm, grad_v, load_sem.at[0])
    pair_load = pltpu.make_async_copy(pair_hbm, pair_v, load_sem.at[1])
    small = [
        pltpu.make_async_copy(src, dst, load_sem.at[2 + n])
        for n, (src, dst) in enumerate(
            ((gain_hbm, gain_ref), (bias_hbm, bias_ref), (w_hbm, w_ref), (mask_hbm, mask_ref))
        )
    ]
    for load in [grad_load, *small, pair_load]:
        load.start()

    peers = []
    for dx, dy, dz in send_order(X, Y, Z):
        px, py, pz = (x + dx) % X, (y + dy) % Y, (z + dz) % Z
        peers.append((pz * 2 + px // 2, py * 2 + px % 2))

    barrier = pltpu.get_barrier_semaphore()
    for prow, pqp in peers:
        pl.semaphore_signal(
            barrier, inc=1, device_id=(prow, pqp * 2 + core), device_id_type=MESH
        )
    pl.semaphore_signal(barrier, inc=1, device_id=(row, qp * 2 + 1 - core), device_id_type=MESH)

    def scatter(n, src_of, dst, own_src):
        pltpu.make_async_copy(own_src, dst, recv_sem.at[n]).start()
        for prow, pqp in peers:
            pltpu.make_async_remote_copy(
                src_ref=src_of(prow, pqp),
                dst_ref=dst,
                send_sem=send_sem.at[n],
                recv_sem=recv_sem.at[n],
                device_id=(prow, pqp * 2 + core),
                device_id_type=MESH,
            ).start()

    def wait_for(ref, sem):
        pltpu.make_async_copy(ref, ref, sem).wait()

    grad_load.wait()

    @pl.loop(0, TJ, unroll=4)
    def _(j):
        f1[pl.ds(j * pitch, H), :] = grad_v[j].astype(F32)

    @pl.loop(0, H, unroll=4)
    def _(c):
        gs[c] = f1[pl.ds(c, TJ, stride=pitch), :].astype(BF16)

    pl.semaphore_wait(barrier, len(peers) + 1)
    lanes = pl.ds(pl.multiple_of(row * TI, TI), TI)
    by_channel = lambda ref: (lambda prow, pqp: ref.at[prow * QP + pqp])
    scatter(0, by_channel(gs), gt.at[qp, pl.ds(pl.multiple_of(core * TJ, TJ), TJ), lanes], gs.at[me])

    for load in small:
        load.wait()
    gain_s[...] = jnp.transpose(jnp.broadcast_to(gain_ref[...], (C, C)))
    bias_s[...] = jnp.transpose(jnp.broadcast_to(bias_ref[...], (C, C)))
    wt_s[...] = jnp.transpose(w_ref[...].astype(F32)).astype(BF16)

    pair_load.wait()

    @pl.loop(0, TI, unroll=4)
    def _(i):
        pair_f[pl.ds(i * pitch, TJ), :] = pair_v[i].astype(F32)

    valid = mask_ref[row, col // 2].astype(F32)
    eye = (
        lax.broadcasted_iota(jnp.int32, (C, C), 0) == lax.broadcasted_iota(jnp.int32, (C, C), 1)
    ).astype(F32).astype(BF16)

    def activate(m, normed, side, f):
        projected = jnp.dot(
            wt_s[pl.ds(2 * side * H, 2 * H), :], normed, preferred_element_type=F32
        )
        lin = projected[0:H]
        sig = jax.nn.sigmoid(projected[H : 2 * H])
        gated = valid * sig
        act[m, pl.ds(2 * side * H, H)] = gated
        act[m, pl.ds((2 * side + 1) * H, H)] = lin * (1.0 - sig)
        activation = gated * lin
        for s in (0, 1):
            f[pl.ds(2 * m + s, H, stride=pitch), :] = activation[:, s * TI : (s + 1) * TI]

    here = (pl.ds(pl.multiple_of(qp * TJ, TJ), TJ), lanes)

    def send_activation(n, f, s, t):
        @pl.loop(0, H, unroll=4)
        def _(c):
            s[c] = f[pl.ds(c * pitch, TJ), :].astype(BF16)

        scatter(n, by_channel(s), t.at[here], s.at[me])

    @pl.loop(0, TJ // 2, unroll=2)
    def _(m):
        tokens = jnp.concatenate(
            [pair_f[pl.ds(2 * m + s, TI, stride=pitch), :] for s in (0, 1)], axis=0
        ).astype(BF16)
        values = lax.dot_general(
            eye, tokens, (((1,), (1,)), ((), ())), preferred_element_type=F32
        )
        centred = values - jnp.mean(values, axis=0, keepdims=True)
        variance = jnp.mean(centred * centred, axis=0, keepdims=True)
        inverse = lax.rsqrt(variance + 1e-05)
        scaled = centred * inverse
        gain = jnp.concatenate([gain_s[...], gain_s[...]], axis=1)
        bias = jnp.concatenate([bias_s[...], bias_s[...]], axis=1)
        normed = (scaled * gain + bias).astype(BF16)
        scaled_s[m] = scaled
        inv_s[m] = jnp.broadcast_to(inverse, (8, 2 * TI))
        normed_s[m] = normed
        activate(m, normed, 0, f2)

    send_activation(1, f2, ls, lt)

    @pl.loop(0, TJ // 2, unroll=2)
    def _(m):
        activate(m, normed_s[m], 1, f3)

    send_activation(2, f3, rs, rt)

    half = gt.at[:, pl.ds(pl.multiple_of(core * TJ, TJ), TJ), :]
    other = gt.at[:, pl.ds(pl.multiple_of((1 - core) * TJ, TJ), TJ), :]
    wait_for(half, recv_sem.at[0])
    share = pltpu.make_async_remote_copy(
        src_ref=half,
        dst_ref=half,
        send_sem=send_sem.at[6],
        recv_sem=recv_sem.at[6],
        device_id=(row, qp * 2 + 1 - core),
        device_id_type=MESH,
    )
    share.start()
    wait_for(other, recv_sem.at[6])

    def block_of(ref):
        return lambda prow, pqp: ref.at[
            pl.ds(pl.multiple_of(pqp * TJ, TJ), TJ), pl.ds(pl.multiple_of(prow * TI, TI), TI)
        ]

    wait_for(lt, recv_sem.at[1])

    @pl.loop(0, RN // 2)
    def _(n):
        g = gt[pl.ds(n * 2, 2)].reshape(2 * TI, RN * TI)
        ogr[:, pl.ds(pl.multiple_of(n * 2 * TI, 2 * TI), 2 * TI)] = lax.dot_general(
            lt[...], g, (((1,), (1,)), ((), ())), preferred_element_type=F32
        ).astype(BF16)

    scatter(3, block_of(ogr), rgr.at[me], block_of(ogr)(row, qp))

    wait_for(rt, recv_sem.at[2])

    @pl.loop(0, RN // 2)
    def _(n):
        cols = pl.ds(pl.multiple_of(n * 2 * TI, 2 * TI), 2 * TI)
        g = gt[:, :, cols].reshape(RN * TI, 2 * TI)
        ogl[:, cols] = jnp.dot(rt[...], g, preferred_element_type=F32).astype(BF16)

    HK = TJ // 2

    def part_of(ref, half_k):
        return lambda prow, pqp: ref.at[
            pl.ds(pl.multiple_of(pqp * TJ + half_k * HK, HK), HK),
            pl.ds(pl.multiple_of(prow * TI, TI), TI),
        ]

    for hk in (0, 1):
        scatter(4 + hk, part_of(ogl, hk), rgl.at[me, pl.ds(hk * HK, HK)], part_of(ogl, hk)(row, qp))

    def grad_proj(f, m, side):
        g = jnp.concatenate([f[pl.ds(2 * m + s, H, stride=pitch), :] for s in (0, 1)], axis=1)
        lin = g * act[m, pl.ds(2 * side * H, H)]
        gate = lin * act[m, pl.ds((2 * side + 1) * H, H)]
        return jnp.concatenate([lin, gate], axis=0).astype(BF16)

    wait_for(rgr, recv_sem.at[3])

    @pl.loop(0, H, unroll=4)
    def _(c):
        f3[pl.ds(c * pitch, TJ), :] = rgr[c].astype(F32)

    @pl.loop(0, TJ // 2, unroll=2)
    def _(m):
        part[m] = jnp.dot(
            w_ref[:, 2 * H : 4 * H], grad_proj(f3, m, 1), preferred_element_type=F32
        )

    for hk in (0, 1):
        wait_for(rgl.at[:, pl.ds(hk * HK, HK)], recv_sem.at[4 + hk])

        @pl.loop(0, H, unroll=4)
        def _(c):
            f2[pl.ds(c * pitch + hk * HK, HK), :] = rgl[c, pl.ds(hk * HK, HK)].astype(F32)

        @pl.loop(hk * HK // 2, (hk + 1) * HK // 2, unroll=2)
        def _(m):
            grad_normed = part[m] + jnp.dot(
                w_ref[:, 0 : 2 * H], grad_proj(f2, m, 0), preferred_element_type=F32
            )
            gain = jnp.concatenate([gain_s[...], gain_s[...]], axis=1)
            scaled = scaled_s[m]
            g = grad_normed * gain
            result = inv_s[m, 0:1] * (
                g
                - jnp.mean(g, axis=0, keepdims=True)
                - scaled * jnp.mean(g * scaled, axis=0, keepdims=True)
            )
            for s in (0, 1):
                pair_f[pl.ds(2 * m + s, TI, stride=pitch), :] = jnp.transpose(
                    result[:, s * TI : (s + 1) * TI]
                )

        @pl.loop(0, TI, unroll=4)
        def _(i):
            out_ref[i, pl.ds(hk * HK, HK)] = pair_f[pl.ds(i * pitch + hk * HK, HK), :].astype(BF16)

    for n, buf in enumerate((gs, ls, rs, rgr)):
        wait_for(buf.at[pl.ds(0, len(peers))], send_sem.at[n])
    for hk in (0, 1):
        rows = pl.ds(hk * HK, HK)
        wait_for(rgl.at[pl.ds(0, len(peers)), rows], send_sem.at[4 + hk])
    wait_for(half, send_sem.at[6])


def shards(RN, QN, pair, grad_x, norm_gain, norm_bias, proj_weight, tile_mask):
    TI, TJ, C = pair.shape
    H = grad_x.shape[2]
    QP = QN // 2
    N = RN * TI
    pitch = TJ + 8
    vmem = lambda *shape: pltpu.VMEM(shape[:-1], shape[-1])
    any_space = pl.BlockSpec(memory_space=pl.ANY)
    in_vmem = pl.BlockSpec(memory_space=pltpu.VMEM)
    out = pl.pallas_call(
        functools.partial(kernel, RN, QN),
        out_shape=pltpu.VMEM((TI, TJ, C), BF16),
        in_specs=[any_space] * 6,
        out_specs=in_vmem,
        scratch_shapes=[
            pltpu.SMEM(tile_mask.shape, jnp.int32),
            vmem(1, C, F32),
            vmem(1, C, F32),
            vmem(C, 4 * H, BF16),
            vmem(TI, TJ, C, BF16),
            vmem(TI * pitch, C, F32),
            vmem(TJ, H, TI, BF16),
            vmem(TJ * pitch, TI, F32),
            vmem(TJ * pitch, TI, F32),
            vmem(TJ * pitch, TI, F32),
            vmem(H, TJ, TI, BF16),
            vmem(H, TJ, TI, BF16),
            vmem(H, TJ, TI, BF16),
            vmem(QP, 2 * TJ, N, BF16),
            vmem(QP * TJ, N, BF16),
            vmem(QP * TJ, N, BF16),
            vmem(QP * TJ, N, BF16),
            vmem(QP * TJ, N, BF16),
            vmem(H, TJ, TI, BF16),
            vmem(H, TJ, TI, BF16),
            vmem(TJ // 2, 4 * H, 2 * TI, F32),
            vmem(TJ // 2, C, 2 * TI, F32),
            vmem(TJ // 2, 8, 2 * TI, F32),
            vmem(TJ // 2, C, 2 * TI, F32),
            vmem(TJ // 2, C, 2 * TI, BF16),
            vmem(4 * H, C, BF16),
            vmem(C, C, F32),
            vmem(C, C, F32),
            pltpu.SemaphoreType.DMA((6,)),
            pltpu.SemaphoreType.DMA((7,)),
            pltpu.SemaphoreType.DMA((7,)),
        ],
        compiler_params=pltpu.CompilerParams(
            collective_id=0, has_side_effects=True, vmem_limit_bytes=60 << 20
        ),
    )(
        tile_mask,
        pair,
        jnp.transpose(grad_x, (1, 2, 0)),
        norm_gain.reshape(1, C),
        norm_bias.reshape(1, C),
        proj_weight,
    )
    return out


def solution(mesh):
    placed = (P("row", "col", None), P("row", "col", None), P(), P(), P(), P())
    body = functools.partial(shards, mesh.shape["row"], mesh.shape["col"])
    return jax.shard_map(
        body, mesh=mesh, in_specs=placed, out_specs=P("row", "col", None), check_vma=False
    )
```
